512 devices in a mesh: gx: 2 (over core), ha: 256 (over z, y, x).
Axes of the slice: x: 4, y: 8, z: 8, core: 2. Of those that a mesh axis runs over, the one named last changes fastest.
Arguments:
- level_set: float32 [768, 160, 256], P('ha', 'gx'), may hold values from -6 to 6
- step_length: float32 [1], replicated, may hold values from 0.12 to 0.2
Outputs:
- level_next: float32 [768, 160, 256], P('ha', 'gx')
The draws below stay inside these ranges and needn't reach their ends.
All inputs are finite; a program needn't handle non-finite values.
Results may differ from the reference program's by a relative error of at most 0.00002.
Values sent between devices are 32-bit elements; how exact they have to be, the bound alone decides.
No kernel may reach another device: no remote copies, remote signals or barrier semaphores. Data moves between devices by JAX's collectives and lax.ppermute only.
A program may use at most 64 MiB of HBM per device.

```python
import jax
import jax.numpy as jnp
from jax import lax

CX = 3
NY = 256
NX = 768
NH = 160


def shard_levels(own_key, extent, split, smallest, largest):
    def one(dim, parts):
        heights = jax.random.uniform(jax.random.fold_in(jax.random.fold_in(own_key, 6), dim), (parts,), jnp.float32, smallest / len(split), largest / len(split))
        return jnp.repeat(jnp.exp(heights), extent[dim] // parts).reshape((-1,) + (1,) * (len(extent) - dim - 1))

    gain = one(*split[0])
    for cut in split[1:]:
        gain = gain * one(*cut)
    return gain


def noise(key, shape, deviation, limit, cuts=(), dtype=jnp.bfloat16):
    factor_of = shard_levels(key, shape, cuts, -0.22, 0.18) if cuts else 1.0
    array = jax.random.normal(key, shape, jnp.float32) * deviation * factor_of
    return jnp.minimum(jnp.maximum(array, -limit), limit).astype(dtype)


def setup_inputs(seed: int = 0) -> dict:
    splits = jax.random.split(jax.random.key(seed), 3)
    return {
        "level_set": noise(splits[0], (NX, NH, NY), 1.0, 6.0, ((0, 256), (1, 2)), jnp.float32),
        "step_length": jnp.clip(jax.random.uniform(splits[1], (1,), jnp.float32, 0.12, 0.2), 0.12, 0.2),
    }


epsilon_weno = 1e-6
speed_rate = 1.0
turn_rate = 1.0


def weno_blend(slope_one, slope_two, slope_three, slope_four, slope_five):
    guess_one = slope_one / 3.0 - 7.0 * slope_two / 6.0 + 11.0 * slope_three / 6.0
    guess_two = -slope_two / 6.0 + 5.0 * slope_three / 6.0 + slope_four / 3.0
    guess_three = slope_three / 3.0 + 5.0 * slope_four / 6.0 - slope_five / 6.0
    smooth_one = 13.0 / 12.0 * (slope_one - 2.0 * slope_two + slope_three) ** 2 + 0.25 * (slope_one - 4.0 * slope_two + 3.0 * slope_three) ** 2
    smooth_two = 13.0 / 12.0 * (slope_two - 2.0 * slope_three + slope_four) ** 2 + 0.25 * (slope_two - slope_four) ** 2
    smooth_three = 13.0 / 12.0 * (slope_three - 2.0 * slope_four + slope_five) ** 2 + 0.25 * (3.0 * slope_three - 4.0 * slope_four + slope_five) ** 2
    weight_one = 0.1 / (smooth_one + epsilon_weno) ** 2
    weight_two = 0.6 / (smooth_two + epsilon_weno) ** 2
    weight_three = 0.3 / (smooth_three + epsilon_weno) ** 2
    weight_sum = weight_one + weight_two + weight_three
    return (weight_one * guess_one + weight_two * guess_two + weight_three * guess_three) / weight_sum


def one_sided(padded, axis, count):
    forward_diff = lax.slice_in_dim(padded, 1, count + 6, axis=axis) - lax.slice_in_dim(padded, 0, count + 5, axis=axis)
    pieces = [lax.slice_in_dim(forward_diff, offset, offset + count, axis=axis) for offset in range(6)]
    minus_side = weno_blend(pieces[0], pieces[1], pieces[2], pieces[3], pieces[4])
    plus_side = weno_blend(pieces[5], pieces[4], pieces[3], pieces[2], pieces[1])
    return minus_side, plus_side


def hamilton_rate(padded, cosine_table, sine_table):
    rows_x = padded.shape[0] - 6
    rows_h = padded.shape[1] - 6
    rows_y = padded.shape[2] - 6
    minus_x, plus_x = one_sided(padded[:, 3:-3, 3:-3], 0, rows_x)
    minus_h, plus_h = one_sided(padded[3:-3, :, 3:-3], 1, rows_h)
    minus_y, plus_y = one_sided(padded[3:-3, 3:-3, :], 2, rows_y)
    cos_grid = cosine_table[None, :, None]
    sin_grid = sine_table[None, :, None]
    hamilton = speed_rate * (cos_grid * (minus_x + plus_x) * 0.5 + sin_grid * (minus_y + plus_y) * 0.5) - turn_rate * jnp.abs((minus_h + plus_h) * 0.5)
    damping = 0.5 * (speed_rate * jnp.abs(cos_grid) * (plus_x - minus_x) + speed_rate * jnp.abs(sin_grid) * (plus_y - minus_y) + turn_rate * (plus_h - minus_h))
    return damping - jnp.maximum(0.0, -hamilton)


def reference(level_set, step_length):
    step_size = step_length[0]
    heading = 2.0 * jnp.pi * jnp.arange(NH).astype(jnp.float32) / NH
    cosine_table = jnp.cos(heading)
    sine_table = jnp.sin(heading)

    def section_rate(section_field):
        padded = jnp.pad(section_field, ((3, 3), (0, 0), (3, 3)))
        padded = jnp.concatenate([padded[:, -3:], padded, padded[:, :3]], axis=1)

        def block_rate(number):
            slab_piece = lax.dynamic_slice_in_dim(padded, number * CX, CX + 6, 0)
            return hamilton_rate(slab_piece, cosine_table, sine_table)

        stacked = lax.map(block_rate, jnp.arange(NX // CX).astype(jnp.int32))
        return stacked.reshape(NX, NH, NY)

    section_one = level_set + step_size * section_rate(level_set)
    section_two = 0.75 * level_set + 0.25 * (section_one + step_size * section_rate(section_one))
    return level_set / 3.0 + (2.0 / 3.0) * (section_two + step_size * section_rate(section_two))
```

```python
import jax
import jax.numpy as jnp
from jax import lax
from jax.sharding import PartitionSpec as P


def weno_pair(d0, d1, d2, d3, d4, d5):
    e0, e1, e2, e3, e4 = d1 - d0, d2 - d1, d3 - d2, d4 - d3, d5 - d4

    def base(e, f):
        t = f - e
        return (13.0 / 3.0) * (t * t) + 4e-6

    def sq(v):
        return v * v

    t0, t1, t2, t3 = base(e0, e1), base(e1, e2), base(e2, e3), base(e3, e4)
    a0 = t0 + sq(3.0 * e1 - e0)
    a1 = t1 + sq(3.0 * e2 - e1)
    b1 = t1 + sq(e1 + e2)
    b2 = t2 + sq(e2 + e3)
    c2 = t2 + sq(3.0 * e2 - e3)
    c3 = t3 + sq(3.0 * e3 - e4)

    def side(s1, s2, s3, q1, q2, q3):
        w1, w2, w3 = sq(s2 * s3), 6.0 * sq(s1 * s3), 3.0 * sq(s1 * s2)
        return (w1 * q1 + w2 * q2 + w3 * q3) / (6.0 * (w1 + w2 + w3))

    minus = d2 + side(a0, b1, c2, 5.0 * e1 - 2.0 * e0, e1 + 2.0 * e2, 4.0 * e2 - e3)
    plus = d3 - side(c3, b2, a1, 5.0 * e3 - 2.0 * e4, e3 + 2.0 * e2, 4.0 * e2 - e1)
    return minus, plus


def one_sided(padded, axis, count):
    d = lax.slice_in_dim(padded, 1, count + 6, axis=axis) - lax.slice_in_dim(padded, 0, count + 5, axis=axis)
    return weno_pair(*[lax.slice_in_dim(d, k, k + count, axis=axis) for k in range(6)])


def on_device(level_set, step_length):
    step = step_length[0]
    rows_x, rows_h, _ = level_set.shape
    count = lax.axis_size("ha")
    even = [p for j in range(0, count - 1, 2) for p in ((j, j + 1), (j + 1, j))]
    odd = [p for j in range(1, count - 1, 2) for p in ((j, j + 1), (j + 1, j))]
    is_odd = lax.axis_index("ha") % 2 == 1
    total_h = lax.axis_size("gx") * rows_h
    global_h = lax.axis_index("gx") * rows_h + jnp.arange(rows_h, dtype=jnp.int32)
    heading = 2.0 * jnp.pi * global_h.astype(jnp.float32) / total_h
    cos_grid = jnp.cos(heading)[None, :, None]
    sin_grid = jnp.sin(heading)[None, :, None]

    def rate(u):
        from_odd = lax.ppermute(u, "ha", odd)
        from_even = lax.ppermute(u, "ha", even)
        edges = jnp.concatenate([u[:, :3], u[:, -3:]], axis=1)
        edges = lax.ppermute(edges, "gx", [(0, 1), (1, 0)])
        minus_y, plus_y = one_sided(jnp.pad(u, ((0, 0), (0, 0), (3, 3))), 2, u.shape[2])
        minus_h, plus_h = one_sided(jnp.concatenate([edges[:, 3:], u, edges[:, :3]], axis=1), 1, rows_h)
        ham = 0.5 * (sin_grid * (minus_y + plus_y) - jnp.abs(minus_h + plus_h))
        damp = 0.5 * (jnp.abs(sin_grid) * (plus_y - minus_y) + (plus_h - minus_h))
        ham, damp = lax.optimization_barrier((ham, damp))
        left = jnp.where(is_odd, from_even, from_odd)
        right = jnp.where(is_odd, from_odd, from_even)
        minus_x, plus_x = one_sided(jnp.concatenate([left, u, right], axis=0), 0, rows_x)
        ham = ham + (0.5 * cos_grid) * (minus_x + plus_x)
        damp = damp + (0.5 * jnp.abs(cos_grid)) * (plus_x - minus_x)
        return damp - jnp.maximum(0.0, -ham)

    one = level_set + step * rate(level_set)
    two = 0.75 * level_set + 0.25 * (one + step * rate(one))
    return level_set / 3.0 + 2.0 / 3.0 * (two + step * rate(two))


def solution(mesh):
    return jax.shard_map(
        on_device,
        mesh=mesh,
        in_specs=(P("ha", "gx", None), P()),
        out_specs=P("ha", "gx", None),
        check_vma=False,
    )
```

```python
import functools

import jax
import jax.numpy as jnp
from jax import lax
from jax.experimental import pallas as pl
from jax.experimental.pallas import tpu as pltpu
from jax.sharding import PartitionSpec as P


def sq(c):
    return c * c


def corrections(e, t, s):
    base = [(13.0 / 3.0) * sq(c) + 4e-6 for c in t]
    triple = [3.0 * c for c in e]
    low = [sq(b + sq(triple[k + 1] - e[k])) for k, b in enumerate(base)]
    mid = [sq(b + sq(e[k] + e[k + 1])) for k, b in enumerate(base)]
    high = [sq(b + sq(triple[k] - e[k + 1])) for k, b in enumerate(base)]

    def shift(first, second, third, outer, inner):
        scaled = 3.0 * first
        twice = third + third
        total = second * third + scaled * (second + twice)
        return second * (twice * outer + scaled * inner) / total

    found = []
    for i in range(len(e) - 4):
        minus = shift(low[i], mid[i + 1], high[i + 2], s[i], s[i + 1])
        plus = shift(high[i + 3], mid[i + 2], low[i + 1], s[i + 2], s[i + 1])
        found.append((minus, plus))
    return found


def line_terms(v):
    d = [b - a for a, b in zip(v, v[1:])]
    e = [b - a for a, b in zip(d, d[1:])]
    t = [b - a for a, b in zip(e, e[1:])]
    s = [b - a for a, b in zip(t, t[1:])]
    terms = []
    for i, (minus, plus) in enumerate(corrections(e, t, s)):
        both = 6.0 * (d[i + 2] + d[i + 3]) + (e[i + 1] - e[i + 3]) + (plus - minus)
        terms.append((both, (plus + minus) - s[i + 1]))
    return terms


LANES = 128


def flat_kernel(u_ref, edge_ref, sin_ref, ham_ref, damp_ref, wide_ref):
    rows_x, rows_h, rows_y = u_ref.shape
    step = rows_h // 8
    tiles = rows_y // LANES
    lane = lax.broadcasted_iota(jnp.int32, (8, LANES), 1)

    def one_row(x, _):
        for c in range(tiles):
            cols = pl.ds(c * LANES, LANES)
            wide_ref[c, 8 : 8 + rows_h, :] = u_ref[x, :, cols]
            wide_ref[c, 5:8, :] = edge_ref[x, 3:6, cols]
            wide_ref[c, 8 + rows_h : 11 + rows_h, :] = edge_ref[x, 0:3, cols]
        for c in range(tiles):
            v = [wide_ref[c, pl.ds(8 + j, 8, stride=step), :] for j in range(-3, step + 3)]
            terms = line_terms(v)
            for j in range(step):
                mine = v[j + 3]

                def moved(k):
                    if k == 0:
                        return mine
                    near = pltpu.roll(mine, (-k) % LANES, 1)
                    other = c - 1 if k < 0 else c + 1
                    if 0 <= other < tiles:
                        far = pltpu.roll(wide_ref[other, pl.ds(8 + j, 8, stride=step), :], (-k) % LANES, 1)
                    else:
                        far = jnp.zeros_like(near)
                    inside = lane >= -k if k < 0 else lane < LANES - k
                    return jnp.where(inside, near, far)

                ((both_y, gap_y),) = line_terms([moved(k) for k in range(-3, 4)])
                both_h, gap_h = terms[j]
                sine = sin_ref[pl.ds(j, 8, stride=step), :]
                rows = pl.ds(j, 8, stride=step)
                ham_ref[x * tiles + c, rows, :] = sine * both_y - jnp.abs(both_h)
                damp_ref[x * tiles + c, rows, :] = jnp.abs(sine) * gap_y + gap_h
        return 0

    lax.fori_loop(0, rows_x, one_row, 0)


def side_kernel(own, kept, parity_ref, step_ref, u_ref, even_ref, odd_ref, ham_ref, damp_ref, cos_ref, first_ref, out_ref):
    rows_x, rows_h, rows_y = u_ref.shape
    flipped = parity_ref[0] == 1
    factor = step_ref[0] * (1.0 / 12.0)
    tiles = rows_y // LANES
    for c in range(tiles):
        cols = pl.ds(c * LANES, LANES)

        def one_group(k, _):
            rows = pl.ds(pl.multiple_of(k * 8, 8), 8)
            even = [even_ref[x, rows, cols] for x in range(rows_x)]
            odd = [odd_ref[x, rows, cols] for x in range(rows_x)]
            mine = [u_ref[x, rows, cols] for x in range(rows_x)]
            left = [jnp.where(flipped, a, b) for a, b in zip(even, odd)]
            right = [jnp.where(flipped, b, a) for a, b in zip(even, odd)]
            cosine = cos_ref[rows, :]
            size = jnp.abs(cosine)
            for x, (both, gap) in enumerate(line_terms(left + mine + right)):
                ham = ham_ref[x * tiles + c, rows, :] + cosine * both
                damp = damp_ref[x * tiles + c, rows, :] + size * gap
                moved = mine[x] + factor * (damp + jnp.minimum(0.0, ham))
                out_ref[x, rows, cols] = own * first_ref[x, rows, cols] + kept * moved if own else moved
            return 0

        lax.fori_loop(0, rows_h // 8, one_group, 0, unroll=5)


def on_device(level_set, step_length):
    rows_x, rows_h, rows_y = level_set.shape
    count = lax.axis_size("ha")
    even_pairs = [p for j in range(0, count - 1, 2) for p in ((j, j + 1), (j + 1, j))]
    odd_pairs = [p for j in range(1, count - 1, 2) for p in ((j, j + 1), (j + 1, j))]
    place = lax.axis_index("ha")
    parity = (place % 2).astype(jnp.int32).reshape(1)
    total_h = lax.axis_size("gx") * rows_h
    global_h = lax.axis_index("gx") * rows_h + jnp.arange(rows_h, dtype=jnp.int32)
    heading = 2.0 * jnp.pi * global_h.astype(jnp.float32) / total_h
    cos_grid = jnp.broadcast_to(jnp.cos(heading)[:, None], (rows_h, LANES))
    sin_grid = jnp.broadcast_to(jnp.sin(heading)[:, None], (rows_h, LANES))
    vmem = pl.BlockSpec(memory_space=pltpu.VMEM)
    smem = pl.BlockSpec(memory_space=pltpu.SMEM)
    block = jax.ShapeDtypeStruct(level_set.shape, jnp.float32)
    half = jax.ShapeDtypeStruct((rows_x * rows_y // LANES, rows_h, LANES), jnp.float32)
    cells = rows_x * rows_h * rows_y

    def even(cells):
        return lax.ppermute(cells, "ha", even_pairs)

    def odd(cells):
        return lax.ppermute(cells, "ha", odd_pairs)

    def turn(field):
        edges = jnp.concatenate([field[:, :3], field[:, -3:]], axis=1)
        return lax.ppermute(edges, "gx", [(0, 1), (1, 0)])

    def flat(field, edges):
        return pl.pallas_call(
            flat_kernel,
            out_shape=(half, half),
            in_specs=[vmem] * 3,
            out_specs=(vmem, vmem),
            scratch_shapes=[pltpu.VMEM((rows_y // LANES, rows_h + 16, LANES), jnp.float32)],
            compiler_params=pltpu.CompilerParams(vmem_limit_bytes=4 << 20),
            cost_estimate=pl.CostEstimate(flops=150 * cells, bytes_accessed=12 * cells, transcendentals=4 * cells),
        )(field, edges, sin_grid)

    def section(field, beside_e, beside_o, terms, own, kept):
        return pl.pallas_call(
            functools.partial(side_kernel, own, kept),
            out_shape=block,
            in_specs=[smem] * 2 + [vmem] * 7,
            out_specs=vmem,
            compiler_params=pltpu.CompilerParams(vmem_limit_bytes=6 << 20),
            cost_estimate=pl.CostEstimate(flops=70 * cells, bytes_accessed=28 * cells, transcendentals=2 * cells),
        )(parity, step_length, field, beside_e, beside_o, *terms, cos_grid, level_set)

    def advance(field, own, kept):
        beside_o = odd(field)
        beside_e = even(field)
        terms = flat(field, turn(field))
        return section(field, beside_e, beside_o, terms, own, kept)

    one = advance(level_set, 0.0, 1.0)
    two = advance(one, 0.75, 0.25)
    return advance(two, 1.0 / 3.0, 2.0 / 3.0)


def solution(mesh):
    return jax.shard_map(
        on_device,
        mesh=mesh,
        in_specs=(P("ha", "gx", None), P()),
        out_specs=P("ha", "gx", None),
        check_vma=False,
    )
```

```python
import functools

import jax
import jax.numpy as jnp
from jax import lax
from jax.experimental import pallas as pl
from jax.experimental.pallas import tpu as pltpu
from jax.sharding import PartitionSpec as P


def sq(c):
    return c * c


def corrections(e, t, s):
    base = [(13.0 / 3.0) * sq(c) + 4e-6 for c in t]
    triple = [3.0 * c for c in e]
    low = [sq(b + sq(triple[k + 1] - e[k])) for k, b in enumerate(base)]
    mid = [sq(b + sq(e[k] + e[k + 1])) for k, b in enumerate(base)]
    high = [sq(b + sq(triple[k] - e[k + 1])) for k, b in enumerate(base)]

    def shift(first, second, third, outer, inner):
        scaled = 3.0 * first
        twice = third + third
        total = second * third + scaled * (second + twice)
        return second * (twice * outer + scaled * inner) / total

    found = []
    for i in range(len(e) - 4):
        minus = shift(low[i], mid[i + 1], high[i + 2], s[i], s[i + 1])
        plus = shift(high[i + 3], mid[i + 2], low[i + 1], s[i + 2], s[i + 1])
        found.append((minus, plus))
    return found


def line_terms(v):
    d = [b - a for a, b in zip(v, v[1:])]
    e = [b - a for a, b in zip(d, d[1:])]
    t = [b - a for a, b in zip(e, e[1:])]
    s = [b - a for a, b in zip(t, t[1:])]
    terms = []
    for i, (minus, plus) in enumerate(corrections(e, t, s)):
        both = 6.0 * (d[i + 2] + d[i + 3]) + (e[i + 1] - e[i + 3]) + (plus - minus)
        terms.append((both, (plus + minus) - s[i + 1]))
    return terms


LANES = 128


def flat_kernel(own, kept, step_ref, u_ref, edge_ref, sin_ref, first_ref, ham_ref, damp_ref, base_ref, wide_ref):
    rows_x, rows_h, rows_y = u_ref.shape
    step = rows_h // 8
    tiles = rows_y // LANES
    lane = lax.broadcasted_iota(jnp.int32, (8, LANES), 1)
    factor = step_ref[0] * (kept / 12.0)

    def one_row(x, _):
        base_ref[x] = own * first_ref[x] + kept * u_ref[x] if own else u_ref[x]
        for c in range(tiles):
            cols = pl.ds(c * LANES, LANES)
            wide_ref[c, 8 : 8 + rows_h, :] = u_ref[x, :, cols]
            wide_ref[c, 5:8, :] = edge_ref[x, 3:6, cols]
            wide_ref[c, 8 + rows_h : 11 + rows_h, :] = edge_ref[x, 0:3, cols]
        for c in range(tiles):
            v = [wide_ref[c, pl.ds(8 + j, 8, stride=step), :] for j in range(-3, step + 3)]
            terms = line_terms(v)
            for j in range(step):
                mine = v[j + 3]

                def moved(k):
                    if k == 0:
                        return mine
                    near = pltpu.roll(mine, (-k) % LANES, 1)
                    other = c - 1 if k < 0 else c + 1
                    if 0 <= other < tiles:
                        far = pltpu.roll(wide_ref[other, pl.ds(8 + j, 8, stride=step), :], (-k) % LANES, 1)
                    else:
                        far = jnp.zeros_like(near)
                    inside = lane >= -k if k < 0 else lane < LANES - k
                    return jnp.where(inside, near, far)

                ((both_y, gap_y),) = line_terms([moved(k) for k in range(-3, 4)])
                both_h, gap_h = terms[j]
                sine = sin_ref[pl.ds(j, 8, stride=step), :]
                rows = pl.ds(j, 8, stride=step)
                ham_ref[x * tiles + c, rows, :] = factor * (sine * both_y - jnp.abs(both_h))
                damp_ref[x * tiles + c, rows, :] = factor * (jnp.abs(sine) * gap_y + gap_h)
        return 0

    lax.fori_loop(0, rows_x, one_row, 0)


def side_kernel(kept, parity_ref, step_ref, u_ref, even_ref, odd_ref, ham_ref, damp_ref, base_ref, cos_ref, out_ref):
    rows_x, rows_h, rows_y = u_ref.shape
    flipped = parity_ref[0] == 1
    factor = step_ref[0] * (kept / 12.0)
    tiles = rows_y // LANES
    for c in range(tiles):
        cols = pl.ds(c * LANES, LANES)

        def one_group(k, _):
            rows = pl.ds(pl.multiple_of(k * 8, 8), 8)
            even = [even_ref[x, rows, cols] for x in range(rows_x)]
            odd = [odd_ref[x, rows, cols] for x in range(rows_x)]
            mine = [u_ref[x, rows, cols] for x in range(rows_x)]
            left = [jnp.where(flipped, a, b) for a, b in zip(even, odd)]
            right = [jnp.where(flipped, b, a) for a, b in zip(even, odd)]
            cosine = factor * cos_ref[rows, :]
            size = jnp.abs(cosine)
            for x, (both, gap) in enumerate(line_terms(left + mine + right)):
                ham = ham_ref[x * tiles + c, rows, :] + cosine * both
                damp = damp_ref[x * tiles + c, rows, :] + size * gap
                out_ref[x, rows, cols] = base_ref[x, rows, cols] + (damp + jnp.minimum(0.0, ham))
            return 0

        lax.fori_loop(0, rows_h // 8, one_group, 0, unroll=5)


def on_device(level_set, step_length):
    rows_x, rows_h, rows_y = level_set.shape
    count = lax.axis_size("ha")
    even_pairs = [p for j in range(0, count - 1, 2) for p in ((j, j + 1), (j + 1, j))]
    odd_pairs = [p for j in range(1, count - 1, 2) for p in ((j, j + 1), (j + 1, j))]
    place = lax.axis_index("ha")
    parity = (place % 2).astype(jnp.int32).reshape(1)
    total_h = lax.axis_size("gx") * rows_h
    global_h = lax.axis_index("gx") * rows_h + jnp.arange(rows_h, dtype=jnp.int32)
    heading = 2.0 * jnp.pi * global_h.astype(jnp.float32) / total_h
    cos_grid = jnp.broadcast_to(jnp.cos(heading)[:, None], (rows_h, LANES))
    sin_grid = jnp.broadcast_to(jnp.sin(heading)[:, None], (rows_h, LANES))
    vmem = pl.BlockSpec(memory_space=pltpu.VMEM)
    smem = pl.BlockSpec(memory_space=pltpu.SMEM)
    block = jax.ShapeDtypeStruct(level_set.shape, jnp.float32)
    half = jax.ShapeDtypeStruct((rows_x * rows_y // LANES, rows_h, LANES), jnp.float32)
    cells = rows_x * rows_h * rows_y

    def even(cells):
        return lax.ppermute(cells, "ha", even_pairs)

    def odd(cells):
        return lax.ppermute(cells, "ha", odd_pairs)

    def turn(field):
        edges = jnp.concatenate([field[:, :3], field[:, -3:]], axis=1)
        return lax.ppermute(edges, "gx", [(0, 1), (1, 0)])

    def flat(field, edges, own, kept):
        return pl.pallas_call(
            functools.partial(flat_kernel, own, kept),
            out_shape=(half, half, block),
            in_specs=[smem] + [vmem] * 4,
            out_specs=(vmem, vmem, vmem),
            scratch_shapes=[pltpu.VMEM((rows_y // LANES, rows_h + 16, LANES), jnp.float32)],
            compiler_params=pltpu.CompilerParams(vmem_limit_bytes=4 << 20),
            cost_estimate=pl.CostEstimate(flops=150 * cells, bytes_accessed=12 * cells, transcendentals=4 * cells),
        )(step_length, field, edges, sin_grid, level_set)

    def section(field, beside_e, beside_o, terms, kept):
        return pl.pallas_call(
            functools.partial(side_kernel, kept),
            out_shape=block,
            in_specs=[smem] * 2 + [vmem] * 7,
            out_specs=vmem,
            compiler_params=pltpu.CompilerParams(vmem_limit_bytes=6 << 20),
            cost_estimate=pl.CostEstimate(flops=70 * cells, bytes_accessed=28 * cells, transcendentals=2 * cells),
        )(parity, step_length, field, beside_e, beside_o, *terms, cos_grid)

    def advance(field, own, kept):
        beside_o = odd(field)
        beside_e = even(field)
        terms = flat(field, turn(field), own, kept)
        return section(field, beside_e, beside_o, terms, kept)

    one = advance(level_set, 0.0, 1.0)
    two = advance(one, 0.75, 0.25)
    return advance(two, 1.0 / 3.0, 2.0 / 3.0)


def solution(mesh):
    return jax.shard_map(
        on_device,
        mesh=mesh,
        in_specs=(P("ha", "gx", None), P()),
        out_specs=P("ha", "gx", None),
        check_vma=False,
    )
```

```python
import functools

import jax
import jax.numpy as jnp
from jax import lax
from jax.experimental import pallas as pl
from jax.experimental.pallas import tpu as pltpu
from jax.sharding import PartitionSpec as P


def sq(c):
    return c * c


def corrections(e, t, s):
    base = [(13.0 / 3.0) * sq(c) + 4e-6 for c in t]
    triple = [3.0 * c for c in e]
    low = [sq(b + sq(triple[k + 1] - e[k])) for k, b in enumerate(base)]
    mid = [sq(b + sq(e[k] + e[k + 1])) for k, b in enumerate(base)]
    high = [sq(b + sq(triple[k] - e[k + 1])) for k, b in enumerate(base)]

    def shift(first, second, third, outer, inner):
        scaled = 3.0 * first
        twice = third + third
        total = second * third + scaled * (second + twice)
        return second * (twice * outer + scaled * inner) / total

    found = []
    for i in range(len(e) - 4):
        minus = shift(low[i], mid[i + 1], high[i + 2], s[i], s[i + 1])
        plus = shift(high[i + 3], mid[i + 2], low[i + 1], s[i + 2], s[i + 1])
        found.append((minus, plus))
    return found


def line_terms(v):
    d = [b - a for a, b in zip(v, v[1:])]
    e = [b - a for a, b in zip(d, d[1:])]
    t = [b - a for a, b in zip(e, e[1:])]
    s = [b - a for a, b in zip(t, t[1:])]
    terms = []
    for i, (minus, plus) in enumerate(corrections(e, t, s)):
        both = 6.0 * (d[i + 2] + d[i + 3]) + (e[i + 1] - e[i + 3]) + (plus - minus)
        terms.append((both, (plus + minus) - s[i + 1]))
    return terms


LANES = 128


def flat_kernel(own, kept, step_ref, u_ref, edge_ref, sin_ref, first_ref, ham_ref, damp_ref, *rest):
    rows_x, rows_h, rows_y = u_ref.shape
    wide_ref = rest[-1]
    step = rows_h // 8
    tiles = rows_y // LANES
    lane = lax.broadcasted_iota(jnp.int32, (8, LANES), 1)
    factor = step_ref[0] * (kept / 12.0)

    def one_row(x, _):
        if own:
            rest[0][x] = own * first_ref[x] + kept * u_ref[x]
        for c in range(tiles):
            cols = pl.ds(c * LANES, LANES)
            wide_ref[c, 8 : 8 + rows_h, :] = u_ref[x, :, cols]
            wide_ref[c, 5:8, :] = edge_ref[x, 3:6, cols]
            wide_ref[c, 8 + rows_h : 11 + rows_h, :] = edge_ref[x, 0:3, cols]
        for c in range(tiles):
            v = [wide_ref[c, pl.ds(8 + j, 8, stride=step), :] for j in range(-3, step + 3)]
            terms = line_terms(v)
            for j in range(step):
                mine = v[j + 3]

                def moved(k):
                    if k == 0:
                        return mine
                    near = pltpu.roll(mine, (-k) % LANES, 1)
                    other = c - 1 if k < 0 else c + 1
                    if 0 <= other < tiles:
                        far = pltpu.roll(wide_ref[other, pl.ds(8 + j, 8, stride=step), :], (-k) % LANES, 1)
                    else:
                        far = jnp.zeros_like(near)
                    inside = lane >= -k if k < 0 else lane < LANES - k
                    return jnp.where(inside, near, far)

                ((both_y, gap_y),) = line_terms([moved(k) for k in range(-3, 4)])
                both_h, gap_h = terms[j]
                sine = sin_ref[pl.ds(j, 8, stride=step), :]
                rows = pl.ds(j, 8, stride=step)
                ham_ref[x * tiles + c, rows, :] = factor * (sine * both_y - jnp.abs(both_h))
                damp_ref[x * tiles + c, rows, :] = factor * (jnp.abs(sine) * gap_y + gap_h)
        return 0

    lax.fori_loop(0, rows_x, one_row, 0)


def side_kernel(kept, parity_ref, step_ref, u_ref, even_ref, odd_ref, ham_ref, damp_ref, base_ref, cos_ref, out_ref):
    rows_x, rows_h, rows_y = u_ref.shape
    flipped = parity_ref[0] == 1
    factor = step_ref[0] * (kept / 12.0)
    tiles = rows_y // LANES
    for c in range(tiles):
        cols = pl.ds(c * LANES, LANES)

        def one_group(k, _):
            rows = pl.ds(pl.multiple_of(k * 8, 8), 8)
            even = [even_ref[x, rows, cols] for x in range(rows_x)]
            odd = [odd_ref[x, rows, cols] for x in range(rows_x)]
            mine = [u_ref[x, rows, cols] for x in range(rows_x)]
            left = [jnp.where(flipped, a, b) for a, b in zip(even, odd)]
            right = [jnp.where(flipped, b, a) for a, b in zip(even, odd)]
            cosine = factor * cos_ref[rows, :]
            size = jnp.abs(cosine)
            for x, (both, gap) in enumerate(line_terms(left + mine + right)):
                ham = ham_ref[x * tiles + c, rows, :] + cosine * both
                damp = damp_ref[x * tiles + c, rows, :] + size * gap
                out_ref[x, rows, cols] = base_ref[x, rows, cols] + (damp + jnp.minimum(0.0, ham))
            return 0

        lax.fori_loop(0, rows_h // 8, one_group, 0, unroll=5)


def on_device(level_set, step_length):
    rows_x, rows_h, rows_y = level_set.shape
    count = lax.axis_size("ha")
    even_pairs = [p for j in range(0, count - 1, 2) for p in ((j, j + 1), (j + 1, j))]
    odd_pairs = [p for j in range(1, count - 1, 2) for p in ((j, j + 1), (j + 1, j))]
    place = lax.axis_index("ha")
    parity = (place % 2).astype(jnp.int32).reshape(1)
    total_h = lax.axis_size("gx") * rows_h
    global_h = lax.axis_index("gx") * rows_h + jnp.arange(rows_h, dtype=jnp.int32)
    heading = 2.0 * jnp.pi * global_h.astype(jnp.float32) / total_h
    cos_grid = jnp.broadcast_to(jnp.cos(heading)[:, None], (rows_h, LANES))
    sin_grid = jnp.broadcast_to(jnp.sin(heading)[:, None], (rows_h, LANES))
    vmem = pl.BlockSpec(memory_space=pltpu.VMEM)
    smem = pl.BlockSpec(memory_space=pltpu.SMEM)
    block = jax.ShapeDtypeStruct(level_set.shape, jnp.float32)
    half = jax.ShapeDtypeStruct((rows_x * rows_y // LANES, rows_h, LANES), jnp.float32)
    cells = rows_x * rows_h * rows_y

    def even(cells):
        return lax.ppermute(cells, "ha", even_pairs)

    def odd(cells):
        return lax.ppermute(cells, "ha", odd_pairs)

    def turn(field):
        edges = jnp.concatenate([field[:, :3], field[:, -3:]], axis=1)
        return lax.ppermute(edges, "gx", [(0, 1), (1, 0)])

    def flat(field, edges, own, kept):
        more = 1 if own else 0
        found = pl.pallas_call(
            functools.partial(flat_kernel, own, kept),
            out_shape=(half, half) + (block,) * more,
            in_specs=[smem] + [vmem] * 4,
            out_specs=(vmem,) * (2 + more),
            scratch_shapes=[pltpu.VMEM((rows_y // LANES, rows_h + 16, LANES), jnp.float32)],
            compiler_params=pltpu.CompilerParams(vmem_limit_bytes=4 << 20),
            cost_estimate=pl.CostEstimate(flops=150 * cells, bytes_accessed=12 * cells, transcendentals=4 * cells),
        )(step_length, field, edges, sin_grid, level_set)
        return found if own else (*found, field)

    def section(field, beside_e, beside_o, terms, kept):
        return pl.pallas_call(
            functools.partial(side_kernel, kept),
            out_shape=block,
            in_specs=[smem] * 2 + [vmem] * 7,
            out_specs=vmem,
            compiler_params=pltpu.CompilerParams(vmem_limit_bytes=6 << 20),
            cost_estimate=pl.CostEstimate(flops=70 * cells, bytes_accessed=28 * cells, transcendentals=2 * cells),
        )(parity, step_length, field, beside_e, beside_o, *terms, cos_grid)

    def advance(field, own, kept):
        beside_o = odd(field)
        beside_e = even(field)
        terms = flat(field, turn(field), own, kept)
        return section(field, beside_e, beside_o, terms, kept)

    one = advance(level_set, 0.0, 1.0)
    two = advance(one, 0.75, 0.25)
    return advance(two, 1.0 / 3.0, 2.0 / 3.0)


def solution(mesh):
    return jax.shard_map(
        on_device,
        mesh=mesh,
        in_specs=(P("ha", "gx", None), P()),
        out_specs=P("ha", "gx", None),
        check_vma=False,
    )
```
